32 devices in a mesh: groups: 2 (over y), ctx: 16 (over z, x, core).
Axes of the slice: x: 2, y: 2, z: 4, core: 2. Of those that a mesh axis runs over, the one named last changes fastest.
Arguments:
- query_vectors: bfloat16 [16384, 2048], P(('groups', 'ctx')), parts along dimension 0, may hold values from -60 to 60
- key_vectors: bfloat16 [16384, 2048], P(('groups', 'ctx')), parts along dimension 0, may hold values from -6 to 6
- value_vectors: bfloat16 [16384, 2048], P(('groups', 'ctx')), parts along dimension 0, may hold values from -8 to 8
- out_weight: bfloat16 [2048, 2048], P(None, 'ctx'), may hold values from -0.125 to 0.125
Outputs:
- projected: bfloat16 [16384, 2048], P(('groups', 'ctx')), parts along dimension 0
The draws below stay inside these ranges and needn't reach their ends.
There are 2 independent parts, one for each index of `groups`. The reference program is written for one: setup_inputs(seed, part) draws one part's arguments, and reference() takes and returns one part's arrays. A program takes and returns all parts, laid end to end along the dimension named above; an argument that names none is the same for every part. Nothing has to cross between parts.
All inputs are finite; a program needn't handle non-finite values.
Results may differ from the reference program's by a relative error of at most 0.0095.
Values may be sent and summed in bfloat16 or wider, within the bound.
No kernel may reach another device: no remote copies, remote signals or barrier semaphores. Data moves between devices by JAX's collectives and lax.ppermute only.
A program may use at most 192 MiB of HBM per device.

```python
import math
import jax
import jax.numpy as jnp
from jax import lax

HEADS = 16
HEAD_DIM = 128
WIDTH = 2048
BLOCK = 128
LEVELS = 5
TOKENS = 8192


def query_key_pair(key):
    base_key = jax.random.fold_in(key, 4321)
    key_query = jax.random.fold_in(base_key, 0)
    key_key = jax.random.fold_in(base_key, 1)
    key_qperiod = jax.random.fold_in(base_key, 5)
    key_qphase = jax.random.fold_in(base_key, 6)
    key_kperiod = jax.random.fold_in(base_key, 7)
    key_kphase = jax.random.fold_in(base_key, 8)
    channels = HEADS * HEAD_DIM
    grid_shape = (TOKENS, channels)
    places = jnp.arange(TOKENS, dtype=jnp.float32)[:, None]
    query_period = jnp.exp(jax.random.uniform(key_qperiod, (1, channels), jnp.float32, math.log(1024.0), math.log(16384.0)))
    query_phase = jax.random.uniform(key_qphase, (1, channels), jnp.float32, -math.pi, math.pi)
    key_period = jnp.exp(jax.random.uniform(key_kperiod, (1, channels), jnp.float32, math.log(256.0), math.log(2048.0)))
    key_phase = jax.random.uniform(key_kphase, (1, channels), jnp.float32, -math.pi, math.pi)
    query_wave = 3.0 * jnp.sin(2.0 * math.pi * places / query_period + query_phase)
    key_wave = 1.5 * jnp.sin(2.0 * math.pi * places / key_period + key_phase)
    key_rows = jnp.clip(jax.random.normal(key_key, grid_shape, jnp.float32), -4.5, 4.5) + key_wave
    query_rows = 2.0 * jnp.clip(jax.random.normal(key_query, grid_shape, jnp.float32), -6.0, 6.0) + query_wave
    return (query_rows, key_rows)


def draw_query_vectors(key, part):
    return query_key_pair(key)[0].astype(jnp.bfloat16)


def draw_key_vectors(key, part):
    return query_key_pair(key)[1].astype(jnp.bfloat16)


def draw_value_vectors(key, part):
    key_rough, key_period, key_phase, key_coarse = jax.random.split(jax.random.fold_in(key, 8765), 4)
    channels = HEADS * HEAD_DIM
    grid_shape = (TOKENS, channels)
    coarse_shape = (TOKENS // 8, channels)
    rough = jnp.clip(jax.random.normal(key_rough, grid_shape, jnp.float32), -6.0, 6.0)
    coarse = 2.5 * jnp.clip(jax.random.normal(key_coarse, coarse_shape, jnp.float32), -3.0, 3.0)
    period = jnp.exp(jax.random.uniform(key_period, (1, channels), jnp.float32, math.log(TOKENS / 16.0), math.log(TOKENS / 2.0)))
    phase = jax.random.uniform(key_phase, (1, channels), jnp.float32, -math.pi, math.pi)
    places = jnp.arange(TOKENS, dtype=jnp.float32)[:, None]
    total = rough + jnp.repeat(coarse, 8, axis=0) + 1.5 * jnp.sin(2.0 * math.pi * places / period + phase)
    return jnp.clip(total, -8.0, 8.0).astype(jnp.bfloat16)


def level_of(stream_key, shape, cuts, smallest, top_value):
    loudness, own = 1.0, jax.random.fold_in(stream_key, 6)
    for axis_at, parts in cuts:
        steps = jnp.exp(jax.random.uniform(jax.random.fold_in(own, axis_at), (parts,), jnp.float32, smallest / len(cuts), top_value / len(cuts)))
        loudness = loudness * jnp.repeat(steps, shape[axis_at] // parts).reshape([-1 if axis == axis_at else 1 for axis in range(len(shape))])
    return loudness


def scatter_about(rng, dims, width, limit, pieces=(), held_as=jnp.bfloat16):
    array = jax.random.normal(rng, dims, jnp.float32) * width
    if len(pieces) > 0:
        array = level_of(rng, dims, pieces, -0.22, 0.18) * array
    return jnp.clip(array, min=-limit, max=limit).astype(held_as)


def setup_inputs(seed: int = 0, part: int = 0) -> dict:
    seeds = jax.random.split(jax.random.key(seed), 5)
    own_keys = jax.random.split(jax.random.fold_in(seeds[4], part), 5)
    query_vectors = draw_query_vectors(jax.random.fold_in(jax.random.fold_in(seeds[4], part), 71), part)
    key_vectors = draw_key_vectors(jax.random.fold_in(jax.random.fold_in(seeds[4], part), 71), part)
    value_vectors = draw_value_vectors(jax.random.fold_in(jax.random.fold_in(seeds[4], part), 71), part)
    out_weight = scatter_about(seeds[3], (HEADS * HEAD_DIM, WIDTH), (HEADS * HEAD_DIM) ** -0.5, 0.125, ((1, 16),))
    return dict(query_vectors=query_vectors, key_vectors=key_vectors, value_vectors=value_vectors, out_weight=out_weight)


def coarsen(matrix):
    paired = matrix.reshape(matrix.shape[0] // 2, 2, matrix.shape[1]).astype(jnp.float32)
    return ((paired[:, 0] + paired[:, 1]) * 0.5).astype(jnp.bfloat16)


def key_valid(height, block_index, row_pos, nblocks):
    grid_shape = (block_index.shape[0], row_pos.shape[0], BLOCK)
    has_left = jnp.broadcast_to((block_index >= 1)[:, None, None], grid_shape)
    has_right = jnp.broadcast_to((block_index + 1 < nblocks)[:, None, None], grid_shape)
    if height == 0:
        return jnp.concatenate([has_left, jnp.ones(grid_shape, jnp.bool_), has_right], axis=2)
    upper_half = (row_pos >= BLOCK // 2)[None, :, None]
    key_place = jnp.arange(BLOCK, dtype=jnp.int32)[None, None, :]
    left_ok = has_left & (upper_half | (key_place < BLOCK // 2))
    right_ok = has_right & (jnp.logical_not(upper_half) | (key_place >= BLOCK // 2))
    return jnp.concatenate([left_ok, right_ok], axis=2)


def level_terms(height, query_rows, key_rows, value_rows):
    score_scale = HEAD_DIM ** -0.5
    nblocks = query_rows.shape[0] // BLOCK
    zero_block = jnp.zeros((1, BLOCK, HEADS, HEAD_DIM), jnp.bfloat16)
    query_blocks = query_rows.reshape(nblocks, BLOCK, HEADS, HEAD_DIM)
    key_padded = jnp.concatenate([zero_block, key_rows.reshape(nblocks, BLOCK, HEADS, HEAD_DIM), zero_block], axis=0)
    value_padded = jnp.concatenate([zero_block, value_rows.reshape(nblocks, BLOCK, HEADS, HEAD_DIM), zero_block], axis=0)
    row_pos = jnp.arange(BLOCK, dtype=jnp.int32)

    def one_block(block_no):
        near_keys = lax.dynamic_slice_in_dim(key_padded, block_no, 3, 0)
        near_values = lax.dynamic_slice_in_dim(value_padded, block_no, 3, 0)
        if height == 0:
            keys_window = near_keys.reshape(3 * BLOCK, HEADS, HEAD_DIM)
            values_window = near_values.reshape(3 * BLOCK, HEADS, HEAD_DIM)
        else:
            keys_window = jnp.concatenate([near_keys[0], near_keys[2]], axis=0)
            values_window = jnp.concatenate([near_values[0], near_values[2]], axis=0)
        admitted = key_valid(height, block_no[None], row_pos, nblocks)[0][None]
        queries = query_blocks[block_no]
        scores = jnp.einsum("rhd,khd->hrk", queries.astype(jnp.float32), keys_window.astype(jnp.float32),
                            precision=lax.Precision.HIGHEST) * score_scale
        scores = jnp.where(admitted, scores, -jnp.inf)
        row_peak = jnp.max(scores, axis=2)
        weights = jnp.where(admitted, jnp.exp(scores - row_peak[:, :, None]), 0.0).astype(jnp.bfloat16)
        numerator = jnp.einsum("hrk,khd->rhd", weights.astype(jnp.float32), values_window.astype(jnp.float32),
                               precision=lax.Precision.HIGHEST)
        denominator = jnp.sum(weights.astype(jnp.float32), axis=2)
        return row_peak.T, numerator, denominator.T

    return lax.map(one_block, jnp.arange(nblocks, dtype=jnp.int32))


def merge_levels(peaks, numerators, denominators):
    spread = [jnp.repeat(peaks[height], 1 << height, axis=0) for height in range(len(peaks))]
    highest = spread[0]
    for level_peak in spread[1:]:
        highest = jnp.maximum(highest, level_peak)
    weighted = 0.0
    normaliser = 0.0
    for height in range(len(peaks)):
        factor = float(1 << height) * jnp.exp(spread[height] - highest)
        weighted = weighted + factor[:, :, None] * jnp.repeat(numerators[height], 1 << height, axis=0)
        normaliser = normaliser + factor * jnp.repeat(denominators[height], 1 << height, axis=0)
    return weighted / normaliser[:, :, None]


def reference(query_vectors, key_vectors, value_vectors, out_weight):
    length = query_vectors.shape[0]
    query_rows, key_rows, value_rows = query_vectors, key_vectors, value_vectors
    peaks, numerators, denominators = [], [], []
    for height in range(LEVELS):
        if height > 0:
            query_rows = coarsen(query_rows)
            key_rows = coarsen(key_rows)
            value_rows = coarsen(value_rows)
        row_peak, numerator, denominator = level_terms(height, query_rows, key_rows, value_rows)
        coarse_rows = length >> height
        peaks.append(row_peak.reshape(coarse_rows, HEADS))
        numerators.append(numerator.reshape(coarse_rows, HEADS, HEAD_DIM))
        denominators.append(denominator.reshape(coarse_rows, HEADS))
    attended = merge_levels(peaks, numerators, denominators).astype(jnp.bfloat16).reshape(length, HEADS * HEAD_DIM)
    return jnp.dot(attended, out_weight, preferred_element_type=jnp.float32).astype(jnp.bfloat16)
```

```python
import math

import jax
import jax.numpy as jnp
from jax import lax
from jax.experimental import pallas as pl
from jax.experimental.pallas import tpu as pltpu
from jax.sharding import PartitionSpec as P

HEAD_DIM = 128
BLOCK = 128
HALF = BLOCK // 2
LOG2 = HEAD_DIM**-0.5 * math.log2(math.e)
MASKED = -1e30
BF16 = jnp.bfloat16
F32 = jnp.float32


def halved(ref, start, rows):
    even = ref[pl.ds(start, rows, stride=2), :]
    odd = ref[pl.ds(start + 1, rows, stride=2), :]
    return ((even + odd) * 0.5).astype(BF16)


def prepare_kernel(info, k_ref, v_ref, x_ref, s_ref, l3_ref, l4_ref, fine):
    odd_core = info[0] == 1
    for side, source in enumerate((k_ref, v_ref)):
        fine[...] = source[...].astype(F32)
        one = halved(fine, 0, 256)
        fine[0:256, :] = one.astype(F32)
        two = halved(fine, 0, 128)
        fine[0:128, :] = two.astype(F32)
        three = halved(fine, 0, 64)
        l3_ref[side] = three
        fine[0:64, :] = three.astype(F32)
        l4_ref[side] = halved(fine, 0, 32)

        def put(low_ref, high_ref):
            low_ref[side, 0:128, :] = source[0:128, :]
            low_ref[side, 128:192, :] = one[64:128]
            low_ref[side, 192:256, :] = two[64:128]
            high_ref[side, 0:128, :] = source[384:512, :]
            high_ref[side, 128:192, :] = one[128:192]
            high_ref[side, 192:256, :] = two[0:64]

        @pl.when(odd_core)
        def _():
            put(s_ref, x_ref)

        @pl.when(jnp.logical_not(odd_core))
        def _():
            put(x_ref, s_ref)


def prepare(info, keys, values):
    rows, channels = keys.shape
    column = pl.BlockSpec((rows, HEAD_DIM), lambda h, info: (0, h))

    def out(n):
        return pl.BlockSpec((2, n, HEAD_DIM), lambda h, info: (0, 0, h))

    def shape(n):
        return jax.ShapeDtypeStruct((2, n, channels), BF16)

    return pl.pallas_call(
        prepare_kernel,
        grid_spec=pltpu.PrefetchScalarGridSpec(
            num_scalar_prefetch=1,
            grid=(channels // HEAD_DIM,),
            in_specs=[column, column],
            out_specs=[out(256), out(256), out(64), out(32)],
            scratch_shapes=[pltpu.VMEM((rows, HEAD_DIM), F32)],
        ),
        out_shape=[shape(256), shape(256), shape(64), shape(32)],
        name="prepare",
    )(info, keys, values)


def third_kernel(info, x_ref, o_ref, fine):
    odd_core = info[0] == 1
    for side in range(2):
        fine[0:128, :] = x_ref[side, 0:128, :].astype(F32)
        one = halved(fine, 0, 64).astype(F32)
        sent_one = x_ref[side, 128:192, :].astype(F32)
        fine[0:64, :] = jnp.where(odd_core, one, sent_one)
        fine[64:128, :] = jnp.where(odd_core, sent_one, one)
        two = halved(fine, 0, 64).astype(F32)
        sent_two = x_ref[side, 192:256, :].astype(F32)
        fine[0:64, :] = jnp.where(odd_core, two, sent_two)
        fine[64:128, :] = jnp.where(odd_core, sent_two, two)
        o_ref[side] = halved(fine, 0, 64)


def third(info, x_halo):
    channels = x_halo.shape[2]
    return pl.pallas_call(
        third_kernel,
        grid_spec=pltpu.PrefetchScalarGridSpec(
            num_scalar_prefetch=1,
            grid=(channels // HEAD_DIM,),
            in_specs=[pl.BlockSpec((2, 256, HEAD_DIM), lambda h, info: (0, 0, h))],
            out_specs=pl.BlockSpec((2, 64, HEAD_DIM), lambda h, info: (0, 0, h)),
            scratch_shapes=[pltpu.VMEM((128, HEAD_DIM), F32)],
        ),
        out_shape=jax.ShapeDtypeStruct((2, 64, channels), BF16),
        name="third",
    )(info, x_halo)


def softmax_block(queries, keys, values, bias=None):
    scores = lax.dot_general(
        queries, keys, (((1,), (1,)), ((), ())), preferred_element_type=F32
    )
    if bias is not None:
        scores = scores + bias
    peak = jnp.max(scores, axis=1, keepdims=True)
    weights = jnp.exp2((scores - peak) * LOG2).astype(BF16)
    both = jnp.dot(weights, values, preferred_element_type=F32)
    peak = jnp.broadcast_to(peak, (peak.shape[0], HEAD_DIM))
    return peak, both[:, :HEAD_DIM], both[:, HEAD_DIM:]


def attend_kernel(
    info, q_ref, k_ref, v_ref, x_ref, s_ref, a_ref, u_ref, d_ref, g_ref, w_ref, o_ref,
    fine, halo, q1, q2, q3, q4, k0, v0, k1, v1, k2, v2, k3, v3, k4, v4, um, uu, uz,
):
    odd_core = info[0] == 1

    @pl.when(pl.program_id(0) == 0)
    def _():
        for ref in (v0, v1, v2, v3, v4):
            ref[:, HEAD_DIM:] = jnp.ones((ref.shape[0], HEAD_DIM), BF16)

    fine[...] = q_ref[...].astype(F32)
    q1[...] = halved(fine, 0, 256)
    fine[0:256, :] = q1[...].astype(F32)
    q2[...] = halved(fine, 0, 128)
    fine[0:128, :] = q2[...].astype(F32)
    q3[...] = halved(fine, 0, 64)
    fine[0:64, :] = q3[...].astype(F32)
    q4[...] = halved(fine, 0, 32)

    for side, (own, z0, z1, z2, z3, z4) in enumerate(
        ((k_ref, k0, k1, k2, k3, k4), (v_ref, v0, v1, v2, v3, v4))
    ):
        lanes = slice(0, HEAD_DIM)
        z0[128:640, lanes] = own[...]
        fine[...] = own[...].astype(F32)
        one = halved(fine, 0, 256)
        z1[0:128, lanes] = one[128:256]
        z1[384:512, lanes] = one[0:128]

        def place(left_ref, right_ref):
            z0[0:128, lanes] = left_ref[side, 0:128, :]
            z0[640:768, lanes] = right_ref[side, 0:128, :]
            halo[0:128, :] = left_ref[side, 0:128, :].astype(F32)
            left_one = halved(halo, 0, 64)
            z1[128:192, lanes] = left_ref[side, 128:192, :]
            z1[192:256, lanes] = left_one
            halo[0:64, :] = left_ref[side, 128:192, :].astype(F32)
            halo[64:128, :] = left_one.astype(F32)
            z2[128:192, lanes] = left_ref[side, 192:256, :]
            z2[192:256, lanes] = halved(halo, 0, 64)
            halo[0:128, :] = right_ref[side, 0:128, :].astype(F32)
            right_one = halved(halo, 0, 64)
            z1[256:320, lanes] = right_one
            z1[320:384, lanes] = right_ref[side, 128:192, :]
            halo[0:64, :] = right_one.astype(F32)
            halo[64:128, :] = right_ref[side, 128:192, :].astype(F32)
            z2[0:64, lanes] = halved(halo, 0, 64)
            z2[64:128, lanes] = right_ref[side, 192:256, :]

        @pl.when(odd_core)
        def _():
            place(s_ref, x_ref)

        @pl.when(jnp.logical_not(odd_core))
        def _():
            place(x_ref, s_ref)

        z3[0:64, lanes] = a_ref[side]
        z3[64:192, lanes] = w_ref[side, 0:128, :]
        z4[0:32, lanes] = u_ref[side]
        z4[32:64, lanes] = d_ref[side]
        z4[64:96, lanes] = g_ref[side]
        z4[96:192, lanes] = w_ref[side, 128:224, :]

    def bias_of(flag):
        return jnp.where(info[flag] == 1, 0.0, MASKED).astype(F32)

    lane = lax.broadcasted_iota(jnp.int32, (1, 192), 1)
    wide = lax.broadcasted_iota(jnp.int32, (1, 384), 1)
    left0, right0 = bias_of(2), bias_of(3)
    first0 = jnp.where(wide < 128, left0, 0.0)
    last0 = jnp.where(wide >= 256, right0, 0.0)

    b4 = lane % 96
    l4, r4, g4 = bias_of(6), bias_of(7), bias_of(8)
    bias4 = jnp.where(b4 < 32, l4, jnp.where(b4 < 64, r4, g4))
    peak, num, den = softmax_block(q4[...], k4[...], v4[...], bias4)

    def widened(level_peak, level_num, level_den, acc, rows):
        for ref, value in zip((um, uu, uz), acc, strict=True):
            ref[pl.ds(0, rows // 2, stride=2), :] = value
            ref[pl.ds(1, rows // 2, stride=2), :] = value
        high = jnp.maximum(level_peak, um[0:rows, :])
        here = jnp.exp2((level_peak - high) * LOG2)
        there = 2.0 * jnp.exp2((um[0:rows, :] - high) * LOG2)
        return (
            high,
            here * level_num + there * uu[0:rows, :],
            here * level_den + there * uz[0:rows, :],
        )

    bias3 = jnp.where(lane < 64, bias_of(4), bias_of(5))
    acc = widened(*softmax_block(q3[...], k3[...], v3[...], bias3), (peak, num, den), 64)

    def stacked(parts):
        return tuple(jnp.concatenate(part, axis=0) for part in zip(*parts, strict=True))

    low2 = jnp.where(lane < 128, right0, left0)
    high2 = jnp.where(lane < 64, right0, left0)
    level = stacked(
        [
            softmax_block(q2[0:64, :], k2[0:192, :], v2[0:192, :], low2),
            softmax_block(q2[64:128, :], k2[64:256, :], v2[64:256, :], high2),
        ]
    )
    acc = widened(*level, acc, 128)

    first_low = jnp.where(lane < 128, 0.0, left0)
    first_high = jnp.where(lane < 64, 0.0, left0)
    last_low = jnp.where(lane < 128, right0, 0.0)
    last_high = jnp.where(lane < 64, right0, 0.0)
    level = stacked(
        [
            softmax_block(q1[0:64, :], k1[0:192, :], v1[0:192, :], first_low),
            softmax_block(q1[64:128, :], k1[64:256, :], v1[64:256, :], first_high),
            softmax_block(q1[128:192, :], k1[256:448, :], v1[256:448, :], last_low),
            softmax_block(q1[192:256, :], k1[320:512, :], v1[320:512, :], last_high),
        ]
    )
    acc = widened(*level, acc, 256)

    for ref, value in zip((um, uu, uz), acc, strict=True):
        ref[pl.ds(0, 256, stride=2), :] = value
        ref[pl.ds(1, 256, stride=2), :] = value
    for block in range(4):
        rows = slice(block * 128, block * 128 + 128)
        window = slice(block * 128, block * 128 + 384)
        bias = first0 if block == 0 else last0 if block == 3 else None
        peak, num, den = softmax_block(q_ref[rows, :], k0[window, :], v0[window, :], bias)
        coarse = um[rows, :]
        high = jnp.maximum(peak, coarse)
        here = jnp.exp2((peak - high) * LOG2)
        there = 2.0 * jnp.exp2((coarse - high) * LOG2)
        total = here * num + there * uu[rows, :]
        norm = here * den + there * uz[rows, :]
        o_ref[rows, :] = (total / norm).astype(BF16)


def attend(info, queries, keys, values, x_halo, s_halo, a, u, d, g, swapped):
    rows, channels = queries.shape
    column = pl.BlockSpec((rows, HEAD_DIM), lambda h, info: (0, h))

    def pair(n):
        return pl.BlockSpec((2, n, HEAD_DIM), lambda h, info: (0, 0, h))

    def k(n):
        return pltpu.VMEM((n, HEAD_DIM), BF16)

    def v(n):
        return pltpu.VMEM((n, 2 * HEAD_DIM), BF16)

    def f(n):
        return pltpu.VMEM((n, HEAD_DIM), F32)

    return pl.pallas_call(
        attend_kernel,
        grid_spec=pltpu.PrefetchScalarGridSpec(
            num_scalar_prefetch=1,
            grid=(channels // HEAD_DIM,),
            in_specs=[column, column, column, pair(256), pair(256), pair(64)]
            + [pair(32), pair(32), pair(32), pair(224)],
            out_specs=column,
            scratch_shapes=[f(512), f(128), k(256), k(128), k(64), k(32)]
            + [k(768), v(768), k(512), v(512), k(256), v(256), k(192), v(192), k(192), v(192)]
            + [f(512), f(512), f(512)],
        ),
        out_shape=jax.ShapeDtypeStruct((rows, channels), BF16),
        name="attend",
    )(info, queries, keys, values, x_halo, s_halo, a, u, d, g, swapped)


def project_kernel(a_ref, w_ref, o_ref):
    weight = jnp.concatenate([w_ref[i] for i in range(w_ref.shape[0])], axis=1)
    o_ref[...] = jnp.dot(a_ref[...], weight, preferred_element_type=F32).astype(BF16)


def project(attended, weight):
    rows, channels = attended.shape
    count, _, width = weight.shape
    step = 4
    return pl.pallas_call(
        project_kernel,
        grid=(count // step,),
        in_specs=[
            pl.BlockSpec((rows, channels), lambda j: (0, 0)),
            pl.BlockSpec((step, channels, width), lambda j: (j, 0, 0)),
        ],
        out_specs=pl.BlockSpec((rows, step * width), lambda j: (0, j)),
        out_shape=jax.ShapeDtypeStruct((rows, count * width), BF16),
        name="project",
    )(attended, weight)


def permuted(block, target):
    n = lax.axis_size("ctx")
    route = [(d, target(d)) for d in range(n) if 0 <= target(d) < n]
    return lax.ppermute(block, "ctx", route)


def per_device(queries, keys, values, out_weight):
    n = lax.axis_size("ctx")
    d = lax.axis_index("ctx")
    core, chip_odd = d % 2, (d // 2) % 2
    left3, right3 = d >= 2, d < n - 2
    left4, right4 = d >= 4, d < n - 4
    info = jnp.stack(
        [
            core,
            chip_odd,
            (d > 0).astype(jnp.int32),
            (d < n - 1).astype(jnp.int32),
            jnp.where(core == 1, right3, left3).astype(jnp.int32),
            jnp.where(core == 1, left3, right3).astype(jnp.int32),
            left4.astype(jnp.int32),
            right4.astype(jnp.int32),
            jnp.where(chip_odd == 1, left4, right4).astype(jnp.int32),
        ]
    )
    x_send, s_send, l3, l4 = prepare(info, keys, values)
    x_halo = permuted(x_send, lambda i: i + 1 if i % 2 else i - 1)
    s_halo = permuted(s_send, lambda i: i ^ 1)
    a = permuted(l3, lambda i: i - 2 if i % 2 else i + 2)
    up = permuted(l4, lambda i: i + 4)
    down = permuted(l4, lambda i: i - 4)
    diagonal = permuted(l4, lambda i: i - 6 if (i // 2) % 2 else i + 6)
    neighbour3 = third(info, x_halo)
    swapped = permuted(
        jnp.concatenate([a, neighbour3, up, down, diagonal], axis=1), lambda i: i ^ 1
    )
    attended = attend(
        info, queries, keys, values, x_halo, s_halo, a, up, down, diagonal, swapped
    )
    width = out_weight.shape[1]
    if width % 128 == 0:
        weight = lax.all_gather(out_weight, "ctx", axis=0)
    else:
        weight = lax.all_gather(out_weight, "ctx", axis=1, tiled=True)
        weight = weight.reshape(weight.shape[0], -1, 128).transpose(1, 0, 2)
    return project(attended, weight)


def solution(mesh):
    rows = P(("groups", "ctx"), None)
    return jax.shard_map(
        per_device,
        mesh=mesh,
        in_specs=(rows, rows, rows, P(None, "ctx")),
        out_specs=rows,
        check_vma=False,
    )
```

```python
import math

import jax
import jax.numpy as jnp
from jax import lax
from jax.experimental import pallas as pl
from jax.experimental.pallas import tpu as pltpu
from jax.sharding import Mesh
from jax.sharding import PartitionSpec as P

HEAD_DIM = 128
BLOCK = 128
HALF = BLOCK // 2
LOG2 = HEAD_DIM**-0.5 * math.log2(math.e)
MASKED = -1e30
BF16 = jnp.bfloat16
F32 = jnp.float32


def halved(ref, start, rows):
    even = ref[pl.ds(start, rows, stride=2), :]
    odd = ref[pl.ds(start + 1, rows, stride=2), :]
    return ((even + odd) * 0.5).astype(BF16)


def prepare_kernel(info, k_ref, v_ref, x_ref, s_ref, one_ref, l3_ref, l4_ref, *scratch):
    odd_core = info[0] == 1
    columns = k_ref.shape[1] // HEAD_DIM
    work = [
        (side, slice(j * HEAD_DIM, (j + 1) * HEAD_DIM), scratch[side * columns + j])
        for side in range(2)
        for j in range(columns)
    ]
    sources = (k_ref, v_ref)
    for side, lanes, fine in work:
        fine[...] = sources[side][:, lanes].astype(F32)
    ones, twos = [], []
    for side, lanes, fine in work:
        ones.append(halved(fine, 0, 256))
        one_ref[side, :, lanes] = ones[-1]
    for (side, lanes, fine), one in zip(work, ones, strict=True):
        fine[0:256, :] = one.astype(F32)
    for side, lanes, fine in work:
        twos.append(halved(fine, 0, 128))
    for (side, lanes, fine), two in zip(work, twos, strict=True):
        fine[0:128, :] = two.astype(F32)
    for side, lanes, fine in work:
        three = halved(fine, 0, 64)
        l3_ref[side, :, lanes] = three
        fine[128:192, :] = three.astype(F32)
    for side, lanes, fine in work:
        l4_ref[side, :, lanes] = halved(fine, 128, 32)

    def put(low_ref, high_ref):
        for (side, lanes, _), one, two in zip(work, ones, twos, strict=True):
            low_ref[side, 0:128, lanes] = sources[side][0:128, lanes]
            low_ref[side, 128:192, lanes] = one[64:128]
            low_ref[side, 192:256, lanes] = two[64:128]
            high_ref[side, 0:128, lanes] = sources[side][384:512, lanes]
            high_ref[side, 128:192, lanes] = one[128:192]
            high_ref[side, 192:256, lanes] = two[0:64]

    @pl.when(odd_core)
    def _():
        put(s_ref, x_ref)

    @pl.when(jnp.logical_not(odd_core))
    def _():
        put(x_ref, s_ref)


def prepare(info, keys, values):
    rows, channels = keys.shape
    wide = 4 * HEAD_DIM
    column = pl.BlockSpec((rows, wide), lambda h, info: (0, h))

    def out(n):
        return pl.BlockSpec((2, n, wide), lambda h, info: (0, 0, h))

    def shape(n):
        return jax.ShapeDtypeStruct((2, n, channels), BF16)

    sizes = (256, 256, 256, 64, 32)
    return pl.pallas_call(
        prepare_kernel,
        grid_spec=pltpu.PrefetchScalarGridSpec(
            num_scalar_prefetch=1,
            grid=(channels // wide,),
            in_specs=[column, column],
            out_specs=[out(n) for n in sizes],
            scratch_shapes=[pltpu.VMEM((rows, HEAD_DIM), F32)] * 8,
        ),
        out_shape=[shape(n) for n in sizes],
        name="prepare",
    )(info, keys, values)


def coarse_kernel(q_ref, q1_ref, q2_ref, q3_ref, q4_ref, *scratch):
    work = [
        (slice(j * HEAD_DIM, (j + 1) * HEAD_DIM), fine) for j, fine in enumerate(scratch)
    ]
    for lanes, fine in work:
        fine[...] = q_ref[:, lanes].astype(F32)
    rows = 256
    for out_ref in (q1_ref, q2_ref, q3_ref, q4_ref):
        for lanes, fine in work:
            value = halved(fine, 0, rows)
            out_ref[:, lanes] = value
            fine[0:rows, :] = value.astype(F32)
        rows //= 2


def coarse(queries):
    rows, channels = queries.shape
    wide = 4 * HEAD_DIM
    sizes = (256, 128, 64, 32)
    return pl.pallas_call(
        coarse_kernel,
        grid=(channels // wide,),
        in_specs=[pl.BlockSpec((rows, wide), lambda h: (0, h))],
        out_specs=[pl.BlockSpec((n, wide), lambda h: (0, h)) for n in sizes],
        out_shape=[jax.ShapeDtypeStruct((n, channels), BF16) for n in sizes],
        scratch_shapes=[pltpu.VMEM((rows, HEAD_DIM), F32)] * 4,
        name="coarse",
    )(queries)


def third_kernel(info, x_ref, one_ref, two_ref, o_ref, *scratch):
    odd_core = info[0] == 1
    columns = x_ref.shape[2] // HEAD_DIM
    work = [
        (side, slice(j * HEAD_DIM, (j + 1) * HEAD_DIM), scratch[side * columns + j])
        for side in range(2)
        for j in range(columns)
    ]
    for side, lanes, fine in work:
        fine[...] = x_ref[side, 0:128, lanes].astype(F32)
    for start, out_ref in ((128, one_ref), (192, two_ref)):
        for side, lanes, fine in work:
            derived = halved(fine, 0, 64)
            sent = x_ref[side, start : start + 64, lanes]
            low = jnp.where(odd_core, derived, sent)
            high = jnp.where(odd_core, sent, derived)
            out_ref[side, 0:64, lanes] = low
            out_ref[side, 64:128, lanes] = high
            fine[0:64, :] = low.astype(F32)
            fine[64:128, :] = high.astype(F32)
    for side, lanes, fine in work:
        o_ref[side, :, lanes] = halved(fine, 0, 64)


def third(info, x_halo):
    channels = x_halo.shape[2]
    wide = 4 * HEAD_DIM

    def pair(n):
        return pl.BlockSpec((2, n, wide), lambda h, info: (0, 0, h))

    return pl.pallas_call(
        third_kernel,
        grid_spec=pltpu.PrefetchScalarGridSpec(
            num_scalar_prefetch=1,
            grid=(channels // wide,),
            in_specs=[pair(256)],
            out_specs=[pair(128), pair(128), pair(64)],
            scratch_shapes=[pltpu.VMEM((128, HEAD_DIM), F32)] * 8,
        ),
        out_shape=[jax.ShapeDtypeStruct((2, n, channels), BF16) for n in (128, 128, 64)],
        name="third",
    )(info, x_halo)


def scores_of(queries, keys):
    return lax.dot_general(
        queries, keys, (((1,), (1,)), ((), ())), preferred_element_type=F32
    )


def softmax_stage(jobs):
    scores = []
    for queries, keys, _, bias in jobs:
        score = scores_of(queries, keys)
        scores.append(score if bias is None else score + bias)
    peaks = [jnp.max(score, axis=1, keepdims=True) for score in scores]
    weights = [
        jnp.exp2((score - peak) * LOG2).astype(BF16)
        for score, peak in zip(scores, peaks, strict=True)
    ]
    results = []
    for (_, _, values, _), weight, peak in zip(jobs, weights, peaks, strict=True):
        both = jnp.dot(weight, values, preferred_element_type=F32)
        peak = jnp.broadcast_to(peak, (peak.shape[0], HEAD_DIM))
        results.append((peak, both[:, :HEAD_DIM], both[:, HEAD_DIM:]))
    return results


def stacked(parts):
    return tuple(jnp.concatenate(part, axis=0) for part in zip(*parts, strict=True))


def spread(refs, acc):
    rows = acc[0].shape[0]
    for ref, value in zip(refs, acc, strict=True):
        ref[pl.ds(0, rows, stride=2), :] = value
        ref[pl.ds(1, rows, stride=2), :] = value


def joined(level, refs, rows):
    peak, num, den = level
    coarse_peak, coarse_num, coarse_den = (ref[rows, :] for ref in refs)
    high = jnp.maximum(peak, coarse_peak)
    here = jnp.exp2((peak - high) * LOG2)
    there = 2.0 * jnp.exp2((coarse_peak - high) * LOG2)
    return (high, here * num + there * coarse_num, here * den + there * coarse_den)


def inner_kernel(info, q_ref, k_ref, v_ref, q1, q2, one_ref, s_ref, *rest):
    size = 14
    scratch = rest[-size * HEADS_PER_STEP :]
    n_ref, l_ref = rest[-size * HEADS_PER_STEP - 2 : -size * HEADS_PER_STEP]
    heads = []
    for j in range(HEADS_PER_STEP):
        own = scratch[size * j : size * j + size]
        heads.append((slice(j * HEAD_DIM, (j + 1) * HEAD_DIM), own[:2], own[2:8], own[8:]))

    @pl.when(pl.program_id(0) == 0)
    def _():
        for _, _, windows, _ in heads:
            for ref in windows[1::2]:
                ref[:, HEAD_DIM:] = jnp.ones((ref.shape[0], HEAD_DIM), BF16)

    lanes = slice(0, HEAD_DIM)
    for cols, fines, windows, _ in heads:
        for side, own in enumerate((k_ref, v_ref)):
            z0, z1, z2 = windows[side::2]
            fine = fines[side]
            near = s_ref[side, 0:128, cols]
            sent_one = s_ref[side, 128:192, cols]
            sent_two = s_ref[side, 192:256, cols]
            z0[0:128, lanes] = near
            z0[128:640, lanes] = own[:, cols]
            z0[640:768, lanes] = near
            z1[0:128, lanes] = one_ref[side, 128:256, cols]
            z1[384:512, lanes] = one_ref[side, 0:128, cols]
            fine[0:128, :] = near.astype(F32)
            derived = halved(fine, 0, 64)
            z1[128:192, lanes] = sent_one
            z1[192:256, lanes] = derived
            z1[256:320, lanes] = derived
            z1[320:384, lanes] = sent_one
            fine[128:192, :] = sent_one.astype(F32)
            fine[192:256, :] = derived.astype(F32)
            fine[256:320, :] = sent_one.astype(F32)
            z2[128:192, lanes] = sent_two
            z2[192:256, lanes] = halved(fine, 128, 64)
            z2[0:64, lanes] = halved(fine, 192, 64)
            z2[64:128, lanes] = sent_two

    left, right = bias_of(info, 0), bias_of(info, 1)
    lane = lax.broadcasted_iota(jnp.int32, (1, 192), 1)
    wide = lax.broadcasted_iota(jnp.int32, (1, 384), 1)
    first0 = jnp.where(wide < 128, left, 0.0)
    last0 = jnp.where(wide >= 256, right, 0.0)
    low2 = jnp.where(lane < 128, right, left)
    high2 = jnp.where(lane < 64, right, left)
    first_low = jnp.where(lane < 128, 0.0, left)
    first_high = jnp.where(lane < 64, 0.0, left)
    last_low = jnp.where(lane < 128, right, 0.0)
    last_high = jnp.where(lane < 64, right, 0.0)
    low, high = slice(0, 192), slice(64, 256)
    jobs = []
    for cols, _, (k0, v0, k1, v1, k2, v2), _ in heads:
        jobs += [
            (q2[0:64, cols], k2[low, :], v2[low, :], low2),
            (q2[64:128, cols], k2[high, :], v2[high, :], high2),
            (q1[0:64, cols], k1[0:192, :], v1[0:192, :], first_low),
            (q1[64:128, cols], k1[64:256, :], v1[64:256, :], first_high),
            (q1[128:192, cols], k1[256:448, :], v1[256:448, :], last_low),
            (q1[192:256, cols], k1[320:512, :], v1[320:512, :], last_high),
        ]
        for block in range(4):
            window = slice(block * 128, block * 128 + 384)
            rows = slice(block * 128, block * 128 + 128)
            bias = first0 if block == 0 else last0 if block == 3 else None
            jobs.append((q_ref[rows, cols], k0[window, :], v0[window, :], bias))
    results = softmax_stage(jobs)
    per_head = [results[10 * j : 10 * j + 10] for j in range(HEADS_PER_STEP)]
    for (_, _, _, refs), done in zip(heads, per_head, strict=True):
        spread(refs[0:3], stacked(done[0:2]))
    for (_, _, _, refs), done in zip(heads, per_head, strict=True):
        spread(refs[3:6], joined(stacked(done[2:6]), refs[0:3], slice(None)))
    for (cols, _, _, refs), done in zip(heads, per_head, strict=True):
        for block in range(4):
            rows = slice(block * 128, block * 128 + 128)
            peak, num, den = joined(done[6 + block], refs[3:6], rows)
            n_ref[rows, cols] = num / den
            l_ref[rows, cols] = peak * LOG2 + jnp.log2(den)


def bias_of(info, flag):
    return jnp.where(info[flag] == 1, 0.0, MASKED).astype(F32)


def k_scratch(n):
    return pltpu.VMEM((n, HEAD_DIM), BF16)


def v_scratch(n):
    return pltpu.VMEM((n, 2 * HEAD_DIM), BF16)


def f_scratch(n):
    return pltpu.VMEM((n, HEAD_DIM), F32)


HEADS_PER_STEP = 2


def column_spec(n, start=0):
    return pl.BlockSpec((n, HEADS_PER_STEP * HEAD_DIM), lambda h, info: (0, start + h))


def pair_spec(n, start=0):
    return pl.BlockSpec((2, n, HEADS_PER_STEP * HEAD_DIM), lambda h, info: (0, 0, start + h))


def inner(info, queries, keys, values, coarse_queries, ones, s_halo, part, parts, earlier):
    rows, channels = queries.shape
    steps = channels // (HEADS_PER_STEP * HEAD_DIM) // parts
    start = part * steps
    in_specs = [column_spec(rows, start)] * 3
    in_specs += [column_spec(256, start), column_spec(128, start)]
    in_specs += [pair_spec(256, start), pair_spec(256, start)]
    operands = [info, queries, keys, values, *coarse_queries[:2], ones, s_halo]
    aliases = {}
    if earlier:
        aliases = {len(operands): 0, len(operands) + 1: 1}
        in_specs += [pl.BlockSpec(memory_space=pl.ANY)] * 2
        operands += earlier
    return pl.pallas_call(
        inner_kernel,
        grid_spec=pltpu.PrefetchScalarGridSpec(
            num_scalar_prefetch=1,
            grid=(steps,),
            in_specs=in_specs,
            out_specs=[column_spec(rows, start)] * 2,
            scratch_shapes=(
                [f_scratch(320), f_scratch(320)]
                + [k_scratch(768), v_scratch(768), k_scratch(512), v_scratch(512)]
                + [k_scratch(256), v_scratch(256)]
                + [f_scratch(n) for n in (256, 512) for _ in range(3)]
            )
            * HEADS_PER_STEP,
        ),
        out_shape=[jax.ShapeDtypeStruct((rows, channels), F32)] * 2,
        input_output_aliases=aliases,
        cost_estimate=pl.CostEstimate(
            flops=1_600_000_000 // parts, bytes_accessed=18_000_000 // parts,
            transcendentals=4_000_000 // parts,
        ),
        name="inner",
    )(*operands)


OUTER_SCRATCH = (
    [v_scratch(n) for n in (192, 192)]
    + [v_scratch(n) for n in (128, 128, 128)]
    + [k_scratch(192), k_scratch(192)]
    + [f_scratch(n) for n in (64, 128, 256, 512, 512, 256) for _ in range(3)]
)


def outer_kernel(
    info, q0, q1, q2, q3, q4, x_ref, one_ref, two_ref, a_ref, u_ref, d_ref, g_ref, w_ref, far_ref,
    n_ref, l_ref, o_ref, *scratch,
):
    odd_core = info[0] == 1
    size = len(OUTER_SCRATCH)
    heads = []
    for j in range(HEADS_PER_STEP):
        own = scratch[size * j : size * j + size]
        heads.append((slice(j * HEAD_DIM, (j + 1) * HEAD_DIM), own[:5], own[5:7], own[7:]))

    @pl.when(pl.program_id(0) == 0)
    def _():
        for _, vs, _, refs in heads:
            for ref in vs:
                ref[:, HEAD_DIM:] = jnp.ones((ref.shape[0], HEAD_DIM), BF16)
            for group, base in ((refs[12:15], MASKED), (refs[15:18], MASKED)):
                for ref, value in zip(group, (base, 0.0, 0.0), strict=True):
                    ref[...] = jnp.full(ref.shape, value, F32)

    lanes = slice(0, HEAD_DIM)
    for cols, (v4, v3, v2, v1, v0), (k4, k3), _ in heads:
        for side, (z4, z3) in enumerate(((k4, k3), (v4, v3))):
            z4[0:32, lanes] = u_ref[side, :, cols]
            z4[32:64, lanes] = d_ref[side, :, cols]
            z4[64:96, lanes] = g_ref[side, :, cols]
            z4[96:192, lanes] = w_ref[side, 64:160, cols]
            z3[0:64, lanes] = a_ref[side, :, cols]
            z3[64:128, lanes] = w_ref[side, 0:64, cols]
            z3[128:192, lanes] = far_ref[side, :, cols]
        v2[:, lanes] = two_ref[1, :, cols]
        v1[:, lanes] = one_ref[1, :, cols]
        v0[:, lanes] = x_ref[1, 0:128, cols]
    missing = bias_of(info, 9)
    row = lax.broadcasted_iota(jnp.int32, (128, 128), 0)
    lane = lax.broadcasted_iota(jnp.int32, (128, 128), 1)
    half = row // HALF
    barred = (half != lane // HALF) & (half == info[0])
    quarter = jnp.where(barred, MASKED, missing)
    lane = lax.broadcasted_iota(jnp.int32, (1, 192), 1)
    b4 = lane % 96
    bias4 = jnp.where(
        b4 < 32, bias_of(info, 6), jnp.where(b4 < 64, bias_of(info, 7), bias_of(info, 8))
    )
    bias3 = jnp.where(lane < 64, bias_of(info, 4), bias_of(info, 5))
    jobs = []
    for cols, (v4, v3, v2, v1, v0), (k4, k3), _ in heads:
        jobs += [
            (q4[:, cols], k4[...], v4[...], bias4),
            (q3[:, cols], k3[...], v3[...], bias3),
            (q2[:, cols], two_ref[0, :, cols], v2[...], quarter),
            (q1[:, cols], one_ref[0, :, cols], v1[...], quarter),
            (q0[:, cols], x_ref[0, 0:128, cols], v0[...], missing),
        ]
    results = softmax_stage(jobs)
    per_head = [results[5 * j : 5 * j + 5] for j in range(HEADS_PER_STEP)]
    edge1 = pl.multiple_of(jnp.where(odd_core, 128, 0), 128)
    edge0 = pl.multiple_of(jnp.where(odd_core, 384, 0), 128)
    every = slice(None)
    for (_, _, _, refs), done in zip(heads, per_head, strict=True):
        spread(refs[0:3], done[0])
        for ref, value in zip(refs[12:15], done[4], strict=True):
            ref[pl.ds(edge0, 128), :] = value
        for ref, value in zip(refs[15:18], done[3], strict=True):
            ref[pl.ds(edge1, 128), :] = value
    for (_, _, _, refs), done in zip(heads, per_head, strict=True):
        spread(refs[3:6], joined(done[1], refs[0:3], every))
    for (_, _, _, refs), done in zip(heads, per_head, strict=True):
        spread(refs[6:9], joined(done[2], refs[3:6], every))
    for _, _, _, refs in heads:
        spread(refs[9:12], joined(tuple(ref[...] for ref in refs[15:18]), refs[6:9], every))
    for cols, _, _, refs in heads:
        for block in range(4):
            rows = slice(block * 128, block * 128 + 128)
            level = tuple(ref[rows, :] for ref in refs[12:15])
            peak, num, den = joined(level, refs[9:12], rows)
            peak = peak * LOG2
            inner_log = l_ref[rows, cols]
            high = jnp.maximum(peak, inner_log)
            here = jnp.exp2(peak - high)
            there = jnp.exp2(inner_log - high)
            total = here * num + there * n_ref[rows, cols]
            o_ref[rows, cols] = (total / (here * den + there)).astype(BF16)


def outer(info, queries, coarse_queries, x_halo, one, two, a, u, d, g, swapped, far, nums, logs):
    rows, channels = queries.shape
    width = HEADS_PER_STEP * HEAD_DIM
    return pl.pallas_call(
        outer_kernel,
        grid_spec=pltpu.PrefetchScalarGridSpec(
            num_scalar_prefetch=1,
            grid=(channels // width,),
            in_specs=[
                pl.BlockSpec((128, width), lambda h, info: (3 * info[0], h)),
                pl.BlockSpec((128, width), lambda h, info: (info[0], h)),
                column_spec(128),
                column_spec(64),
                column_spec(32),
            ]
            + [pair_spec(n) for n in (256, 128, 128, 64, 32, 32, 32, 160, 64)]
            + [column_spec(rows), column_spec(rows)],
            out_specs=column_spec(rows),
            scratch_shapes=OUTER_SCRATCH * HEADS_PER_STEP,
        ),
        out_shape=jax.ShapeDtypeStruct((rows, channels), BF16),
        cost_estimate=pl.CostEstimate(
            flops=400_000_000, bytes_accessed=16_000_000, transcendentals=2_000_000
        ),
        name="outer",
    )(
        info, queries, *coarse_queries, x_halo, one, two, a, u, d, g, swapped, far, nums, logs
    )


def project_kernel(a_ref, w_ref, o_ref):
    weight = jnp.concatenate([w_ref[i] for i in range(w_ref.shape[0])], axis=1)
    o_ref[...] = jnp.dot(a_ref[...], weight, preferred_element_type=F32).astype(BF16)


def project(attended, weight):
    rows, channels = attended.shape
    count, _, width = weight.shape
    step = 4
    return pl.pallas_call(
        project_kernel,
        grid=(count // step,),
        in_specs=[
            pl.BlockSpec((rows, channels), lambda j: (0, 0)),
            pl.BlockSpec((step, channels, width), lambda j: (j, 0, 0)),
        ],
        out_specs=pl.BlockSpec((rows, step * width), lambda j: (0, j)),
        out_shape=jax.ShapeDtypeStruct((rows, count * width), BF16),
        name="project",
    )(attended, weight)


def gathered_project_kernel(where, a_ref, w_ref, o_ref):
    half = a_ref.shape[1] // 2
    x = where[0]
    for other_x in range(2):
        total = None
        for y in range(2):
            part = jnp.concatenate([w_ref[y, 0, 0, other_x], w_ref[y, 0, 1, other_x]], axis=1)
            product = jnp.dot(
                a_ref[:, y * half : (y + 1) * half], part, preferred_element_type=F32
            )
            total = product if total is None else total + product
        lane = pl.multiple_of((x if other_x == 0 else 1 - x) * 256, 256)
        o_ref[:, pl.ds(lane, 256)] = total.astype(BF16)


def gathered_project(where, attended, weight):
    rows, channels = attended.shape
    shape = weight.shape
    return pl.pallas_call(
        gathered_project_kernel,
        grid_spec=pltpu.PrefetchScalarGridSpec(
            num_scalar_prefetch=1,
            grid=(shape[1],),
            in_specs=[
                pl.BlockSpec((rows, channels), lambda i, where: (0, 0)),
                pl.BlockSpec((shape[0], 1, *shape[2:]), lambda i, where: (0, i, 0, 0, 0, 0)),
            ],
            out_specs=pl.BlockSpec((rows, channels // shape[1]), lambda i, where: (0, i)),
        ),
        out_shape=jax.ShapeDtypeStruct((rows, channels), BF16),
        cost_estimate=pl.CostEstimate(
            flops=2 * rows * channels * channels, bytes_accessed=12_000_000, transcendentals=0
        ),
        name="project",
    )(where, attended, weight)


PARTS = 1
CTX = ("z", "x", "c")


def permuted(block, target):
    n = lax.axis_size(CTX)
    route = [(d, target(d)) for d in range(n) if 0 <= target(d) < n]
    return lax.ppermute(block, CTX, route)


def layer(queries, keys, values, out_weight):
    n = lax.axis_size(CTX)
    d = lax.axis_index(CTX)
    core, chip_odd = d % 2, (d // 2) % 2
    left3, right3 = d >= 2, d < n - 2
    left4, right4 = d >= 4, d < n - 4
    info = jnp.stack(
        [
            core,
            1 - core,
            core,
            core,
            jnp.where(core == 1, right3, left3).astype(jnp.int32),
            jnp.where(core == 1, left3, right3).astype(jnp.int32),
            left4.astype(jnp.int32),
            right4.astype(jnp.int32),
            jnp.where(chip_odd == 1, left4, right4).astype(jnp.int32),
            jnp.where(core == 1, d < n - 1, d > 0).astype(jnp.int32),
        ]
    )
    channels, width = out_weight.shape
    by_links = width == 128 and lax.axis_size("y") == 2 and lax.axis_size("x") == 2
    if by_links:
        rows = channels // 2
        half = lax.dynamic_slice_in_dim(out_weight, lax.axis_index("y") * rows, rows, 0)
        across = lax.ppermute(half, "x", [(0, 1), (1, 0)])
        weight = lax.all_gather(jnp.stack([half, across]), ("y", "z", "c"), axis=0)
        weight = weight.reshape(2, -1, 2, 2, rows, width)
    else:
        weight = lax.all_gather(out_weight, CTX, axis=1, tiled=True)
        weight = weight.reshape(channels, -1, 128).transpose(1, 0, 2)
    x_send, s_send, ones, l3, l4 = prepare(info, keys, values)
    x_halo = permuted(x_send, lambda i: i + 1 if i % 2 else i - 1)
    s_halo = permuted(s_send, lambda i: i ^ 1)
    a = permuted(l3, lambda i: i - 2 if i % 2 else i + 2)
    up = permuted(l4, lambda i: i + 4)
    down = permuted(l4, lambda i: i - 4)
    diagonal = permuted(l4, lambda i: i - 6 if (i // 2) % 2 else i + 6)
    coarse_queries = coarse(queries)
    state = ()
    for part in range(PARTS):
        state = inner(info, queries, keys, values, coarse_queries, ones, s_halo, part, PARTS, state)
    swapped = permuted(jnp.concatenate([a, up, down, diagonal], axis=1), lambda i: i ^ 1)
    one, two, three = third(info, x_halo)
    far = permuted(three, lambda i: i ^ 1)
    attended = outer(
        info, queries, coarse_queries, x_halo, one, two, a, up, down, diagonal, swapped, far, *state
    )
    if by_links:
        return gathered_project(lax.axis_index("x")[None], attended, weight)
    return project(attended, weight)


def solution(mesh):
    groups, n = mesh.devices.shape
    across = 2 ** ((n // 2).bit_length() // 3)
    grid = Mesh(mesh.devices.reshape(groups, n // (2 * across), across, 2), ("y", *CTX))
    rows = P(("y", *CTX), None)
    return jax.shard_map(
        layer,
        mesh=grid,
        in_specs=(rows, rows, rows, P(None, CTX)),
        out_specs=rows,
        check_vma=False,
    )
```
